512 devices in a mesh: section: 16 (over y_hi, x, core), expert: 32 (over z, y_lo).
Axes of the slice: x: 4, y: 4 (y_hi: 2, y_lo: 2; y = y_hi * 2 + y_lo), z: 16, core: 2. Of those that a mesh axis runs over, the one named last changes fastest.
Arguments:
- ahead_rows: bfloat16 [16, 384, 7168], P('section', None, 'expert'), may hold values from -6 to 6
- behind_rows: bfloat16 [16, 384, 7168], P('section', None, 'expert'), may hold values from -6 to 6
- behind_grad: bfloat16 [16, 384, 7168], P('section', None, 'expert'), may hold values from -6 to 6
- route_scores: float32 [16, 2, 384], P('section'), may hold values from 0.1 to 1
- route_counts: int32 [16, 2], P('section'), may hold values from 96 to 384, as said below
- gate_up: bfloat16 [16, 32, 2, 256, 1792], P('section', 'expert'), may hold values from -0.0625 to 0.0625
- down_proj: bfloat16 [16, 32, 256, 1792], P('section', 'expert'), may hold values from -0.125 to 0.125
Outputs:
- ahead_sent: bfloat16 [16, 384, 7168], P('section', None, 'expert')
- behind_sent: bfloat16 [16, 384, 7168], P('section', None, 'expert')
The draws below stay inside these ranges and needn't reach their ends.
Inputs may be any that keep to these rules, and one draw needn't show every extreme that they name: `route_counts`: live slots of each section's expert per micro-batch; in each micro-batch some section has all 384 slots live.
All inputs are finite; a program needn't handle non-finite values.
Results may differ from the reference program's by a relative error of at most 0.02.
Values may be sent and summed in bfloat16 or wider, within the bound.
A program may use at most 64 MiB of HBM per device.

```python
import math
import jax
import jax.numpy as jnp
from jax import lax

D = 7168
FF = 2048
CAP = 384
DBLOCKS = 4
FGROUPS = 8
UNITS = 256
QWIDTH = 1792
N_SECTION = 16
N_EXPERT = 32


def draw_route_counts(key, part):
    first_key, second_key = jax.random.split(jax.random.fold_in(key, 11))
    base = jax.random.randint(first_key, (N_SECTION, 2), CAP // 4, CAP + 1)
    chosen = jax.random.randint(second_key, (2,), 0, N_SECTION)
    sections = jnp.arange(N_SECTION, dtype=jnp.int32)[:, None]
    return jnp.where(sections == chosen[None, :], CAP, base).astype(jnp.int32)


def block_levels(stream_key, dims, pieces, least, top_value):
    def one(position, shards_of):
        steps = jax.random.uniform(jax.random.fold_in(jax.random.fold_in(stream_key, 6), position), (shards_of,), jnp.float32, least / len(pieces), top_value / len(pieces))
        return jnp.repeat(jnp.exp(steps), dims[position] // shards_of).reshape((-1,) + (1,) * (len(dims) - position - 1))

    factor_of = one(*pieces[0])
    for cut in pieces[1:]:
        factor_of = factor_of * one(*cut)
    return factor_of


def scatter_about(own_key, dims, scale, bound, cuts=(), kind=jnp.bfloat16):
    array = jax.random.normal(own_key, dims, jnp.float32) * scale
    if len(cuts) > 0:
        array = block_levels(own_key, dims, cuts, -0.22, 0.18) * array
    return jnp.clip(array, min=-bound, max=bound).astype(kind)


def setup_inputs(seed: int = 0) -> dict:
    splits = jax.random.split(jax.random.key(seed), 8)
    ahead_rows = scatter_about(splits[0], (N_SECTION, CAP, D), 1.0, 6.0, ((0, 16), (2, 32)))
    behind_rows = scatter_about(splits[1], (N_SECTION, CAP, D), 1.0, 6.0, ((0, 16), (2, 32)))
    behind_grad = scatter_about(splits[2], (N_SECTION, CAP, D), 1.0, 6.0, ((0, 16), (2, 32)))
    route_scores = jnp.clip(jnp.exp(math.log(1.0) - 2.3025851 * jax.random.uniform(splits[3], (N_SECTION, 2, CAP), jnp.float32) ** block_levels(splits[3], (N_SECTION, 2, CAP), ((0, 16),), -0.2, 0.2)), 0.1, 1.0)
    route_counts = draw_route_counts(jax.random.fold_in(splits[7], 71), 0)
    gate_up = scatter_about(splits[5], (N_SECTION, N_EXPERT, 2, UNITS, QWIDTH), D ** -0.5, 0.0625, ((0, 16), (1, 32)))
    down_proj = scatter_about(splits[6], (N_SECTION, N_EXPERT, UNITS, QWIDTH), FF ** -0.5, 0.125, ((0, 16), (1, 32)))
    return {"ahead_rows": ahead_rows, "behind_rows": behind_rows, "behind_grad": behind_grad, "route_scores": route_scores, "route_counts": route_counts, "gate_up": gate_up, "down_proj": down_proj}


def silu_float(value):
    return value * jax.nn.sigmoid(value)


def expand_inner(tiles):
    blocks = tiles.astype(jnp.float32).reshape(DBLOCKS, FGROUPS, 2, UNITS, QWIDTH)
    return jnp.transpose(blocks, (2, 1, 3, 0, 4)).reshape(2, FF, D)


def expand_outer(tiles):
    blocks = tiles.astype(jnp.float32).reshape(DBLOCKS, FGROUPS, UNITS, QWIDTH)
    return jnp.transpose(blocks, (1, 2, 0, 3)).reshape(FF, D)


def section_pass(operands):
    ahead, behind, grad_in, scores, counts, gate_tiles, down_tiles = operands
    slots = jnp.arange(CAP, dtype=jnp.int32)
    scale_ahead = scores[0] * (slots < counts[0]).astype(jnp.float32)
    scale_behind = scores[1] * (slots < counts[1]).astype(jnp.float32)
    gate_wide = expand_inner(gate_tiles)
    down_wide = expand_outer(down_tiles)
    scaled_grad = (grad_in.astype(jnp.float32) * scale_behind[:, None]).astype(jnp.bfloat16)
    pre_ahead = jnp.einsum("cd,kfd->ckf", ahead.astype(jnp.float32), gate_wide)
    pre_behind = jnp.einsum("cd,kfd->ckf", behind.astype(jnp.float32), gate_wide)
    expanded = jnp.einsum("cd,fd->cf", scaled_grad.astype(jnp.float32), down_wide)
    hidden = (silu_float(pre_ahead[:, 0]) * pre_ahead[:, 1]).astype(jnp.bfloat16)
    gate_val = pre_behind[:, 0]
    up_val = pre_behind[:, 1]
    sigmoid_gate = jax.nn.sigmoid(gate_val)
    grad_gate = (expanded * up_val * sigmoid_gate * (1.0 + gate_val * (1.0 - sigmoid_gate))).astype(jnp.bfloat16)
    grad_up = (expanded * gate_val * sigmoid_gate).astype(jnp.bfloat16)
    summed_ahead = jnp.einsum("cf,fd->cd", hidden.astype(jnp.float32), down_wide)
    ahead_out = (summed_ahead * scale_ahead[:, None]).astype(jnp.bfloat16)
    stacked = jnp.stack([grad_gate, grad_up], axis=1).astype(jnp.float32)
    behind_out = jnp.einsum("ckf,kfd->cd", stacked, gate_wide).astype(jnp.bfloat16)
    return ahead_out, behind_out


def reference(ahead_rows, behind_rows, behind_grad, route_scores, route_counts, gate_up, down_proj):
    ahead_out, behind_out = lax.map(section_pass, (ahead_rows, behind_rows, behind_grad, route_scores, route_counts, gate_up, down_proj))
    blank = jnp.zeros_like(ahead_out[:1])
    ahead_sent = jnp.concatenate([blank, ahead_out[:-1]], axis=0)
    behind_sent = jnp.concatenate([behind_out[1:], blank], axis=0)
    return (ahead_sent, behind_sent)
```

```python
import functools

import jax
import jax.numpy as jnp
from jax import lax
from jax.experimental import pallas as pl
from jax.experimental.pallas import tpu as pltpu
from jax.sharding import PartitionSpec as P

MESH = pl.DeviceIdType.MESH
DBLOCKS = 4
LINE = 4
CHUNK = 128
F32 = jnp.float32
BF16 = jnp.bfloat16


def layer_kernel(
    chunks, sections, xin, gate_up, down, scale, out_ref,
    xall, wt, pf, pb, rs_in, rl_out, actb, oacc, obf, y_in, zl_send, zr_send, zl_in, zr_in, fin, landed, fsum,
    ag_send, ag_recv, rs_send, rs_recv, aq_send, aq_recv, y_send, y_recv, z_send, z_recv, s_send, s_recv,
):
    feats = xin.shape[1]
    units = down.shape[0]
    half = units // (2 * DBLOCKS)
    me = lax.axis_index("expert")
    sec = lax.axis_index("section")
    devices = lax.axis_size("expert")
    col = me % 2
    z = me // 2
    line = z % LINE
    q = z // LINE
    q_up, q_down = (q + 1) % DBLOCKS, (q + 3) % DBLOCKS

    def expert(index):
        return {"expert": index % devices}

    right, left = expert(me + 2), expert(me + devices - 2)
    across = {"expert": z * 2 + (1 - col)}
    ahead_q, back_q = expert(me + 2 * LINE), expert(me + devices - 2 * LINE)
    sec_up = {"section": (sec + 1) % sections}
    sec_down = {"section": (sec + sections - 1) % sections}

    barrier = pltpu.get_barrier_semaphore()
    for peer in (right, left, across, ahead_q, back_q, sec_up, sec_down):
        pl.semaphore_signal(barrier, inc=1, device_id=peer, device_id_type=MESH)
    pl.semaphore_wait(barrier, 7)

    drains = []

    def remote(src, dst, send, recv, device):
        return pltpu.make_async_remote_copy(
            src_ref=src, dst_ref=dst, send_sem=send, recv_sem=recv, device_id=device, device_id_type=MESH
        )

    def post(copy, cond=None):
        if cond is None:
            copy.start()
        else:
            pl.when(cond)(lambda: copy.start())
        drains.append((copy, cond))

    def arrived(ref, recv):
        remote(ref, ref, recv, recv, across).wait_recv()

    def rows_of(position, column):
        return pl.ds(pl.multiple_of((position * 2 + column) * feats, 16), feats)

    def slot_of(position, column):
        return position * 2 + column

    def gather_own(j):
        spot = xall.at[j, rows_of(line, col), :]
        sem = ag_recv.at[j, slot_of(line, col)]
        post(remote(xin.at[j], spot, ag_send.at[j, 0], sem, right), line < LINE - 1)
        post(remote(xin.at[j], spot, ag_send.at[j, 1], sem, left), line > 0)
        post(remote(xin.at[j], spot, ag_send.at[j, 2], sem, across))
        xall[j, rows_of(line, col), :] = xin[j]

    def gather_step(j, t):
        for side in (0, 1):
            there = line >= t if side == 0 else line + t < LINE
            source = (line - t) & 3 if side == 0 else (line + t) & 3
            spot = xall.at[j, rows_of(source, col), :]
            sem = ag_recv.at[j, slot_of(source, col)]
            pl.when(there)(functools.partial(arrived, spot, sem))
            if t < LINE - 1:
                onward = jnp.logical_and(there, line < LINE - 1 if side == 0 else line > 0)
                post(remote(spot, spot, ag_send.at[j, 3 * t + side], sem, right if side == 0 else left), onward)
            post(remote(spot, spot, ag_send.at[j, 12 + 2 * t + side], sem, across), there)

    def gather_rest(j):
        for position in range(LINE):
            arrived(xall.at[j, rows_of(position, 1 - col), :], ag_recv.at[j, slot_of(position, 1 - col)])

    def first_matmul(j):
        def keep(value, comp):
            for block in range(DBLOCKS):
                for part in range(2):
                    rows = value[(2 * block + part) * half : (2 * block + part + 1) * half]
                    pf[j, block, part, comp] = rows
                    pb[j, block, part, comp] = rows.astype(BF16)

        for k in range(2):
            value = jnp.dot(gate_up[k], xall[j, :, : 2 * CHUNK], preferred_element_type=F32)
            keep(value[:, :CHUNK], k)
            keep(value[:, CHUNK:], 2 + k)
        keep(jnp.dot(down[...], xall[j, :, 2 * CHUNK :], preferred_element_type=F32), 4)

    def sums_start(j):
        across_q = (q + 2) % DBLOCKS
        post(remote(pb.at[j, across_q, 1], rs_in.at[j, 1], rs_send.at[j, 1], rs_recv.at[j, 1], ahead_q))
        post(remote(pb.at[j, across_q, 0], rs_in.at[j, 3], rs_send.at[j, 3], rs_recv.at[j, 3], back_q))
        post(remote(pb.at[j, q_up, 0], rs_in.at[j, 0], rs_send.at[j, 0], rs_recv.at[j, 0], ahead_q))
        post(remote(pb.at[j, q_down, 1], rs_in.at[j, 2], rs_send.at[j, 2], rs_recv.at[j, 2], back_q))

    def sums_relay(j):
        arrived(rs_in.at[j, 1], rs_recv.at[j, 1])
        rl_out[j, 0] = (pf[j, q_up, 1] + rs_in[j, 1].astype(F32)).astype(BF16)
        post(remote(rl_out.at[j, 0], rs_in.at[j, 4], rs_send.at[j, 4], rs_recv.at[j, 4], ahead_q))
        arrived(rs_in.at[j, 3], rs_recv.at[j, 3])
        rl_out[j, 1] = (pf[j, q_down, 0] + rs_in[j, 3].astype(F32)).astype(BF16)
        post(remote(rl_out.at[j, 1], rs_in.at[j, 5], rs_send.at[j, 5], rs_recv.at[j, 5], back_q))

    def activate(j):
        for part, direct, relayed in ((0, 0, 5), (1, 2, 4)):
            arrived(rs_in.at[j, direct], rs_recv.at[j, direct])
            arrived(rs_in.at[j, relayed], rs_recv.at[j, relayed])
            total = pf[j, q, part] + rs_in[j, direct].astype(F32) + rs_in[j, relayed].astype(F32)
            gate_a, up_a, gate_b, up_b, expanded = [total[k] for k in range(5)]
            actb[j, q, part, 0] = (gate_a * jax.nn.sigmoid(gate_a) * up_a).astype(BF16)
            sg = jax.nn.sigmoid(gate_b)
            actb[j, q, part, 1] = (expanded * up_b * sg * (1.0 + gate_b * (1.0 - sg))).astype(BF16)
            actb[j, q, part, 2] = (expanded * gate_b * sg).astype(BF16)
        own = actb.at[j, q]
        post(remote(own, own, aq_send.at[j, 0], aq_recv.at[j, 0], ahead_q))
        post(remote(own, own, aq_send.at[j, 1], aq_recv.at[j, 1], back_q))

    def acts_relay(j):
        arrived(actb.at[j, q_down], aq_recv.at[j, 0])
        piece = actb.at[j, q_down, 0]
        post(remote(piece, piece, aq_send.at[j, 2], aq_recv.at[j, 2], ahead_q))
        arrived(actb.at[j, q_up], aq_recv.at[j, 1])
        piece = actb.at[j, q_up, 1]
        post(remote(piece, piece, aq_send.at[j, 3], aq_recv.at[j, 3], back_q))

    def second_matmul(j):
        far = (q + 2) % DBLOCKS
        arrived(actb.at[j, far, 0], aq_recv.at[j, 2])
        arrived(actb.at[j, far, 1], aq_recv.at[j, 3])
        acts = [actb[j, :, :, k].reshape(units, CHUNK) for k in range(3)]
        both = 2 * feats

        @pl.loop(0, LINE)
        def _(position):
            rows = pl.ds(pl.multiple_of(position * both, 16), both)
            ahead = jnp.dot(wt[2, rows, :], acts[0], preferred_element_type=F32)
            behind = jnp.dot(wt[0, rows, :], acts[1], preferred_element_type=F32)
            behind += jnp.dot(wt[1, rows, :], acts[2], preferred_element_type=F32)
            oacc[j, 0, rows, :] = ahead
            oacc[j, 1, rows, :] = behind
            obf[j, 0, rows, :] = ahead.astype(BF16)
            obf[j, 1, rows, :] = behind.astype(BF16)

        for position in (0, 3, 1, 2):
            post(
                remote(
                    obf.at[j, :, rows_of(position, 1 - col), :], y_in.at[j, position],
                    y_send.at[j, position], y_recv.at[j, position], across,
                )
            )

    def column_sum(j, position):
        return oacc[j, :, rows_of(position, col), :] + y_in[j, position].astype(F32)

    def scatter_line(j, t):
        for side in (0, 1):
            target = LINE - 1 - t if side == 0 else t
            sends = line < target if side == 0 else line > target
            inner = line > 0 if side == 0 else line < LINE - 1
            joins = jnp.logical_and(sends, inner)
            landing, sending = (zr_in, zr_send) if side == 0 else (zl_in, zl_send)
            if t < LINE // 2:
                arrived(y_in.at[j, target], y_recv.at[j, target])

            @pl.when(jnp.logical_and(sends, jnp.logical_not(inner)))
            def _():
                sending[j, target] = column_sum(j, target).astype(BF16)

            @pl.when(joins)
            def _():
                arrived(landing.at[j, target], z_recv.at[j, side, target])
                sending[j, target] = (column_sum(j, target) + landing[j, target].astype(F32)).astype(BF16)

            post(
                remote(
                    sending.at[j, target], landing.at[j, target], z_send.at[j, side, target],
                    z_recv.at[j, side, target], right if side == 0 else left,
                ),
                sends,
            )

    def finish(j):
        fsum[...] = column_sum(j, line)
        for side in (0, 1):
            landing = zr_in if side == 0 else zl_in

            @pl.when(line > 0 if side == 0 else line < LINE - 1)
            def _():
                arrived(landing.at[j, line], z_recv.at[j, side, line])
                fsum[...] += landing[j, line].astype(F32)

        fin[j, 0] = (fsum[0] * scale[j]).astype(BF16)
        fin[j, 1] = fsum[1].astype(BF16)
        post(remote(fin.at[j, 0], landed.at[j, 0], s_send.at[j, 0], s_recv.at[j, 0], sec_up), sec < sections - 1)
        post(remote(fin.at[j, 1], landed.at[j, 1], s_send.at[j, 1], s_recv.at[j, 1], sec_down), sec > 0)

    def deliver(j):
        for k, there in ((0, sec > 0), (1, sec < sections - 1)):

            @pl.when(there)
            def _():
                arrived(landed.at[j, k], s_recv.at[j, k])
                out_ref[k, j] = landed[j, k]

            @pl.when(jnp.logical_not(there))
            def _():
                out_ref[k, j] = jnp.zeros_like(landed[j, k])

    gather_own(0)
    gather_own(1)
    for k in range(2):
        wt[k] = gate_up[k].T
    wt[2] = down[...].T
    for t in (1, 2, 3):
        gather_step(0, t)
    gather_own(2)
    gather_rest(0)
    first_matmul(0)
    sums_start(0)
    for t in (1, 2, 3):
        gather_step(1, t)
    sums_relay(0)
    gather_rest(1)
    first_matmul(1)
    sums_start(1)
    activate(0)
    for t in (1, 2, 3):
        gather_step(2, t)
    sums_relay(1)
    acts_relay(0)
    gather_rest(2)
    first_matmul(2)
    sums_start(2)
    second_matmul(0)
    activate(1)
    sums_relay(2)
    for t in range(LINE - 1):
        scatter_line(0, t)
    acts_relay(1)
    second_matmul(1)
    activate(2)
    finish(0)
    acts_relay(2)
    for t in range(LINE - 1):
        scatter_line(1, t)
    second_matmul(2)
    finish(1)
    for t in range(LINE - 1):
        scatter_line(2, t)
    finish(2)
    for j in range(chunks):
        deliver(j)
    for copy, cond in drains:
        if cond is None:
            copy.wait_send()
        else:
            pl.when(cond)(lambda copy=copy: copy.wait_send())


def body(sections, ahead_rows, behind_rows, behind_grad, route_scores, route_counts, gate_up, down_proj):
    weights_in = gate_up[0, 0]
    weights_out = down_proj[0, 0]
    _, units, width = weights_in.shape
    slots, feats = ahead_rows.shape[1:]
    chunks = slots // CHUNK
    half = units // (2 * DBLOCKS)
    slot_ids = jnp.arange(slots, dtype=jnp.int32)
    scale_ahead = route_scores[0, 0] * (slot_ids < route_counts[0, 0]).astype(F32)
    scale_behind = route_scores[0, 1] * (slot_ids < route_counts[0, 1]).astype(F32)
    scaled_grad = (behind_grad[0].astype(F32) * scale_behind[:, None]).astype(BF16)
    rows = jnp.stack([ahead_rows[0], behind_rows[0], scaled_grad]).reshape(3, chunks, CHUNK, feats)
    xin = rows.transpose(1, 3, 0, 2).reshape(chunks, feats, 3 * CHUNK)
    vmem = pl.BlockSpec(memory_space=pltpu.VMEM)
    dma = pltpu.SemaphoreType.DMA
    piece = (5, half, CHUNK)
    out = pl.pallas_call(
        functools.partial(layer_kernel, chunks, sections),
        out_shape=jax.ShapeDtypeStruct((2, chunks, feats, CHUNK), BF16),
        in_specs=[vmem] * 4,
        out_specs=vmem,
        scratch_shapes=[
            pltpu.VMEM((chunks, width, 3 * CHUNK), BF16),
            pltpu.VMEM((3, width, units), BF16),
            pltpu.VMEM((chunks, DBLOCKS, 2) + piece, F32),
            pltpu.VMEM((chunks, DBLOCKS, 2) + piece, BF16),
            pltpu.VMEM((chunks, 6) + piece, BF16),
            pltpu.VMEM((chunks, 2) + piece, BF16),
            pltpu.VMEM((chunks, DBLOCKS, 2, 3, half, CHUNK), BF16),
            pltpu.VMEM((chunks, 2, width, CHUNK), F32),
            pltpu.VMEM((chunks, 2, width, CHUNK), BF16),
            pltpu.VMEM((chunks, LINE, 2, feats, CHUNK), BF16),
            pltpu.VMEM((chunks, LINE, 2, feats, CHUNK), BF16),
            pltpu.VMEM((chunks, LINE, 2, feats, CHUNK), BF16),
            pltpu.VMEM((chunks, LINE, 2, feats, CHUNK), BF16),
            pltpu.VMEM((chunks, LINE, 2, feats, CHUNK), BF16),
            pltpu.VMEM((chunks, 2, feats, CHUNK), BF16),
            pltpu.VMEM((chunks, 2, feats, CHUNK), BF16),
            pltpu.VMEM((2, feats, CHUNK), F32),
            dma((chunks, 20)),
            dma((chunks, 2 * LINE)),
            dma((chunks, 6)),
            dma((chunks, 6)),
            dma((chunks, 4)),
            dma((chunks, 4)),
            dma((chunks, LINE)),
            dma((chunks, LINE)),
            dma((chunks, 2, LINE)),
            dma((chunks, 2, LINE)),
            dma((chunks, 2)),
            dma((chunks, 2)),
        ],
        compiler_params=pltpu.CompilerParams(
            collective_id=0, has_side_effects=True, vmem_limit_bytes=56 * 1024 * 1024
        ),
        name="routed_layer",
    )(xin, weights_in, weights_out, scale_ahead.reshape(chunks, 1, CHUNK))
    moved = out.transpose(0, 1, 3, 2).reshape(2, slots, feats)
    return (moved[0][None], moved[1][None])


def solution(mesh):
    in_specs = (
        P("section", None, "expert"),
        P("section", None, "expert"),
        P("section", None, "expert"),
        P("section", None, None),
        P("section", None),
        P("section", "expert", None, None, None),
        P("section", "expert", None, None),
    )
    out_specs = (P("section", None, "expert"), P("section", None, "expert"))
    step = functools.partial(body, mesh.shape["section"])
    return jax.shard_map(step, mesh=mesh, in_specs=in_specs, out_specs=out_specs, check_vma=False)
```

```python
import functools

import jax
import jax.numpy as jnp
from jax import lax
from jax.experimental import pallas as pl
from jax.experimental.pallas import tpu as pltpu
from jax.sharding import PartitionSpec as P

MESH = pl.DeviceIdType.MESH
DBLOCKS = 4
LINE = 4
CHUNK = 128
F32 = jnp.float32
BF16 = jnp.bfloat16


def layer_kernel(
    chunks, sections, ahead, behind, grad, scores, counts, gate_up, down, out_ahead, out_behind,
    w, xall, wt, pf, pb, rs_in, rl_out, actb, oacc, obf, y_in, zl_send, zr_send, zl_in, zr_in, fin, landed, fsum,
    w_sem, ag_send, ag_recv, rs_send, rs_recv, aq_send, aq_recv, y_send, y_recv, z_send, z_recv, s_send, s_recv,
):
    feats = ahead.shape[0]
    units = down.shape[0]
    half = units // (2 * DBLOCKS)
    me = lax.axis_index("expert")
    sec = lax.axis_index("section")
    devices = lax.axis_size("expert")
    col = me % 2
    z = me // 2
    line = z % LINE
    q = z // LINE
    q_up, q_down = (q + 1) % DBLOCKS, (q + 3) % DBLOCKS

    def expert(index):
        return {"expert": index % devices}

    right, left = expert(me + 2), expert(me + devices - 2)
    across = {"expert": z * 2 + (1 - col)}
    ahead_q, back_q = expert(me + 2 * LINE), expert(me + devices - 2 * LINE)
    sec_up = {"section": (sec + 1) % sections}
    sec_down = {"section": (sec + sections - 1) % sections}

    loads = [pltpu.make_async_copy(gate_up.at[k], w.at[k], w_sem.at[k]) for k in range(2)]
    loads.append(pltpu.make_async_copy(down, w.at[2], w_sem.at[2]))
    for load in loads:
        load.start()
    barrier = pltpu.get_barrier_semaphore()
    for peer in (right, left, across, ahead_q, back_q, sec_up, sec_down):
        pl.semaphore_signal(barrier, inc=1, device_id=peer, device_id_type=MESH)

    drains = []

    def remote(src, dst, send, recv, device):
        return pltpu.make_async_remote_copy(
            src_ref=src, dst_ref=dst, send_sem=send, recv_sem=recv, device_id=device, device_id_type=MESH
        )

    def post(copy, cond=None):
        if cond is None:
            copy.start()
        else:
            pl.when(cond)(lambda: copy.start())
        drains.append((copy, cond))

    def arrived(ref, recv):
        remote(ref, ref, recv, recv, across).wait_recv()

    def rows_of(position, column):
        return pl.ds(pl.multiple_of((position * 2 + column) * feats, 16), feats)

    def slot_of(position, column):
        return position * 2 + column

    def scale_of(m, j):
        slots = lax.broadcasted_iota(jnp.int32, (1, CHUNK), 1) + j * CHUNK
        return jnp.where(slots < counts[m], scores[m : m + 1, j * CHUNK : (j + 1) * CHUNK], 0.0)

    def place_own(j):
        slots = slice(j * CHUNK, (j + 1) * CHUNK)
        mine = rows_of(line, col)
        xall[j, mine, :CHUNK] = ahead[:, slots]
        xall[j, mine, CHUNK : 2 * CHUNK] = behind[:, slots]
        xall[j, mine, 2 * CHUNK :] = (grad[:, slots].astype(F32) * scale_of(1, j)).astype(BF16)

    def gather_own(j):
        spot = xall.at[j, rows_of(line, col), :]
        sem = ag_recv.at[j, slot_of(line, col)]
        post(remote(spot, spot, ag_send.at[j, 0], sem, right), line < LINE - 1)
        post(remote(spot, spot, ag_send.at[j, 1], sem, left), line > 0)
        post(remote(spot, spot, ag_send.at[j, 2], sem, across))

    def gather_step(j, t):
        for side in (0, 1):
            there = line >= t if side == 0 else line + t < LINE
            source = (line - t) & 3 if side == 0 else (line + t) & 3
            spot = xall.at[j, rows_of(source, col), :]
            sem = ag_recv.at[j, slot_of(source, col)]
            pl.when(there)(functools.partial(arrived, spot, sem))
            if t < LINE - 1:
                onward = jnp.logical_and(there, line < LINE - 1 if side == 0 else line > 0)
                post(remote(spot, spot, ag_send.at[j, 3 * t + side], sem, right if side == 0 else left), onward)
            post(remote(spot, spot, ag_send.at[j, 12 + 2 * t + side], sem, across), there)

    def gather_step1(j):
        gather_step(j, 1)

    def gather_step2(j):
        gather_step(j, 2)

    def gather_step3(j):
        gather_step(j, 3)

    def gather_rest(j):
        for position in range(LINE):
            arrived(xall.at[j, rows_of(position, 1 - col), :], ag_recv.at[j, slot_of(position, 1 - col)])

    def first_matmul(j):
        def keep(value, comp):
            for block in range(DBLOCKS):
                for part in range(2):
                    rows = value[(2 * block + part) * half : (2 * block + part + 1) * half]
                    pf[j, block, part, comp] = rows
                    pb[j, block, part, comp] = rows.astype(BF16)

        for k in range(2):
            value = jnp.dot(w[k], xall[j, :, : 2 * CHUNK], preferred_element_type=F32)
            keep(value[:, :CHUNK], k)
            keep(value[:, CHUNK:], 2 + k)
        keep(jnp.dot(w[2], xall[j, :, 2 * CHUNK :], preferred_element_type=F32), 4)

    def sums_start(j):
        across_q = (q + 2) % DBLOCKS
        post(remote(pb.at[j, across_q, 1], rs_in.at[j, 1], rs_send.at[j, 1], rs_recv.at[j, 1], ahead_q))
        post(remote(pb.at[j, across_q, 0], rs_in.at[j, 3], rs_send.at[j, 3], rs_recv.at[j, 3], back_q))
        post(remote(pb.at[j, q_up, 0], rs_in.at[j, 0], rs_send.at[j, 0], rs_recv.at[j, 0], ahead_q))
        post(remote(pb.at[j, q_down, 1], rs_in.at[j, 2], rs_send.at[j, 2], rs_recv.at[j, 2], back_q))

    def sums_relay(j):
        arrived(rs_in.at[j, 1], rs_recv.at[j, 1])
        rl_out[j, 0] = (pf[j, q_up, 1] + rs_in[j, 1].astype(F32)).astype(BF16)
        post(remote(rl_out.at[j, 0], rs_in.at[j, 4], rs_send.at[j, 4], rs_recv.at[j, 4], ahead_q))
        arrived(rs_in.at[j, 3], rs_recv.at[j, 3])
        rl_out[j, 1] = (pf[j, q_down, 0] + rs_in[j, 3].astype(F32)).astype(BF16)
        post(remote(rl_out.at[j, 1], rs_in.at[j, 5], rs_send.at[j, 5], rs_recv.at[j, 5], back_q))

    def activate(j):
        for part, direct, relayed in ((0, 0, 5), (1, 2, 4)):
            arrived(rs_in.at[j, direct], rs_recv.at[j, direct])
            arrived(rs_in.at[j, relayed], rs_recv.at[j, relayed])
            total = pf[j, q, part] + rs_in[j, direct].astype(F32) + rs_in[j, relayed].astype(F32)
            gate_a, up_a, gate_b, up_b, expanded = [total[k] for k in range(5)]
            actb[j, q, part, 0] = (gate_a * jax.nn.sigmoid(gate_a) * up_a).astype(BF16)
            sg = jax.nn.sigmoid(gate_b)
            actb[j, q, part, 1] = (expanded * up_b * sg * (1.0 + gate_b * (1.0 - sg))).astype(BF16)
            actb[j, q, part, 2] = (expanded * gate_b * sg).astype(BF16)
        own = actb.at[j, q]
        post(remote(own, own, aq_send.at[j, 0], aq_recv.at[j, 0], ahead_q))
        post(remote(own, own, aq_send.at[j, 1], aq_recv.at[j, 1], back_q))

    def acts_relay(j):
        arrived(actb.at[j, q_down], aq_recv.at[j, 0])
        piece = actb.at[j, q_down, 0]
        post(remote(piece, piece, aq_send.at[j, 2], aq_recv.at[j, 2], ahead_q))
        arrived(actb.at[j, q_up], aq_recv.at[j, 1])
        piece = actb.at[j, q_up, 1]
        post(remote(piece, piece, aq_send.at[j, 3], aq_recv.at[j, 3], back_q))

    def second_matmul(j):
        far = (q + 2) % DBLOCKS
        arrived(actb.at[j, far, 0], aq_recv.at[j, 2])
        arrived(actb.at[j, far, 1], aq_recv.at[j, 3])
        acts = [actb[j, :, :, k].reshape(units, CHUNK) for k in range(3)]
        both = 2 * feats

        @pl.loop(0, LINE)
        def _(position):
            rows = pl.ds(pl.multiple_of(position * both, 16), both)
            ahead = jnp.dot(wt[2, rows, :], acts[0], preferred_element_type=F32)
            behind = jnp.dot(wt[0, rows, :], acts[1], preferred_element_type=F32)
            behind += jnp.dot(wt[1, rows, :], acts[2], preferred_element_type=F32)
            oacc[j, 0, rows, :] = ahead
            oacc[j, 1, rows, :] = behind
            obf[j, 0, rows, :] = ahead.astype(BF16)
            obf[j, 1, rows, :] = behind.astype(BF16)

        for position in (0, 3, 1, 2):
            post(
                remote(
                    obf.at[j, :, rows_of(position, 1 - col), :], y_in.at[j, position],
                    y_send.at[j, position], y_recv.at[j, position], across,
                )
            )

    def column_sum(j, position):
        return oacc[j, :, rows_of(position, col), :] + y_in[j, position].astype(F32)

    def scatter_line(j):
        for t in range(LINE - 1):
            scatter_target(j, t)

    def scatter_target(j, t):
        for side in (0, 1):
            target = LINE - 1 - t if side == 0 else t
            sends = line < target if side == 0 else line > target
            inner = line > 0 if side == 0 else line < LINE - 1
            joins = jnp.logical_and(sends, inner)
            landing, sending = (zr_in, zr_send) if side == 0 else (zl_in, zl_send)
            if t < LINE // 2:
                arrived(y_in.at[j, target], y_recv.at[j, target])

            @pl.when(jnp.logical_and(sends, jnp.logical_not(inner)))
            def _():
                sending[j, target] = column_sum(j, target).astype(BF16)

            @pl.when(joins)
            def _():
                arrived(landing.at[j, target], z_recv.at[j, side, target])
                sending[j, target] = (column_sum(j, target) + landing[j, target].astype(F32)).astype(BF16)

            post(
                remote(
                    sending.at[j, target], landing.at[j, target], z_send.at[j, side, target],
                    z_recv.at[j, side, target], right if side == 0 else left,
                ),
                sends,
            )

    def finish(j):
        fsum[...] = column_sum(j, line)
        for side in (0, 1):
            landing = zr_in if side == 0 else zl_in

            @pl.when(line > 0 if side == 0 else line < LINE - 1)
            def _():
                arrived(landing.at[j, line], z_recv.at[j, side, line])
                fsum[...] += landing[j, line].astype(F32)

        fin[j, 0] = (fsum[0] * scale_of(0, j)).astype(BF16)
        fin[j, 1] = fsum[1].astype(BF16)
        post(remote(fin.at[j, 0], landed.at[j, 0], s_send.at[j, 0], s_recv.at[j, 0], sec_up), sec < sections - 1)
        post(remote(fin.at[j, 1], landed.at[j, 1], s_send.at[j, 1], s_recv.at[j, 1], sec_down), sec > 0)

    def deliver(j):
        slots = slice(j * CHUNK, (j + 1) * CHUNK)
        for k, there, out in ((0, sec > 0, out_ahead), (1, sec < sections - 1, out_behind)):

            @pl.when(there)
            def _():
                arrived(landed.at[j, k], s_recv.at[j, k])
                out[:, slots] = landed[j, k]

            @pl.when(jnp.logical_not(there))
            def _():
                out[:, slots] = jnp.zeros((feats, CHUNK), BF16)

    def enter(j):
        gather_rest(j)
        first_matmul(j)
        sums_start(j)

    place_own(1)
    pl.semaphore_wait(barrier, 7)
    gather_own(1)
    place_own(2)
    gather_own(2)
    place_own(0)
    for k in range(3):
        loads[k].wait()
        wt[k] = w[k].T
    for step, j in (
        (gather_step1, 1), (gather_own, 0), (gather_step2, 1), (gather_step3, 1), (gather_step1, 0),
        (gather_step2, 0), (gather_step1, 2), (gather_step3, 0), (enter, 1), (gather_step2, 2), (enter, 0),
        (sums_relay, 1), (sums_relay, 0), (activate, 1), (gather_step3, 2), (enter, 2), (activate, 0),
        (sums_relay, 2), (acts_relay, 0), (activate, 2), (acts_relay, 1), (second_matmul, 0), (acts_relay, 2),
        (second_matmul, 1), (scatter_line, 0), (second_matmul, 2), (scatter_line, 1), (finish, 0),
        (scatter_line, 2), (finish, 1), (finish, 2), (deliver, 1), (deliver, 0), (deliver, 2),
    ):
        step(j)
    for copy, cond in drains:
        if cond is None:
            copy.wait_send()
        else:
            pl.when(cond)(lambda copy=copy: copy.wait_send())


def body(sections, ahead_rows, behind_rows, behind_grad, route_scores, route_counts, gate_up, down_proj):
    weights_in = gate_up[0, 0]
    weights_out = down_proj[0, 0]
    _, units, width = weights_in.shape
    slots, feats = ahead_rows.shape[1:]
    chunks = slots // CHUNK
    half = units // (2 * DBLOCKS)
    vmem = pl.BlockSpec(memory_space=pltpu.VMEM)
    smem = pl.BlockSpec(memory_space=pltpu.SMEM)
    here = pl.BlockSpec(memory_space=pl.ANY)
    dma = pltpu.SemaphoreType.DMA
    out = jax.ShapeDtypeStruct((feats, slots), BF16)
    piece = (5, half, CHUNK)
    moved = pl.pallas_call(
        functools.partial(layer_kernel, chunks, sections),
        out_shape=(out, out),
        in_specs=[vmem, vmem, vmem, vmem, smem, here, here],
        out_specs=(vmem, vmem),
        scratch_shapes=[
            pltpu.VMEM((3, units, width), BF16),
            pltpu.VMEM((chunks, width, 3 * CHUNK), BF16),
            pltpu.VMEM((3, width, units), BF16),
            pltpu.VMEM((chunks, DBLOCKS, 2) + piece, F32),
            pltpu.VMEM((chunks, DBLOCKS, 2) + piece, BF16),
            pltpu.VMEM((chunks, 6) + piece, BF16),
            pltpu.VMEM((chunks, 2) + piece, BF16),
            pltpu.VMEM((chunks, DBLOCKS, 2, 3, half, CHUNK), BF16),
            pltpu.VMEM((chunks, 2, width, CHUNK), F32),
            pltpu.VMEM((chunks, 2, width, CHUNK), BF16),
            pltpu.VMEM((chunks, LINE, 2, feats, CHUNK), BF16),
            pltpu.VMEM((chunks, LINE, 2, feats, CHUNK), BF16),
            pltpu.VMEM((chunks, LINE, 2, feats, CHUNK), BF16),
            pltpu.VMEM((chunks, LINE, 2, feats, CHUNK), BF16),
            pltpu.VMEM((chunks, LINE, 2, feats, CHUNK), BF16),
            pltpu.VMEM((chunks, 2, feats, CHUNK), BF16),
            pltpu.VMEM((chunks, 2, feats, CHUNK), BF16),
            pltpu.VMEM((2, feats, CHUNK), F32),
            dma((3,)),
            dma((chunks, 20)),
            dma((chunks, 2 * LINE)),
            dma((chunks, 6)),
            dma((chunks, 6)),
            dma((chunks, 4)),
            dma((chunks, 4)),
            dma((chunks, LINE)),
            dma((chunks, LINE)),
            dma((chunks, 2, LINE)),
            dma((chunks, 2, LINE)),
            dma((chunks, 2)),
            dma((chunks, 2)),
        ],
        compiler_params=pltpu.CompilerParams(
            collective_id=0, has_side_effects=True, vmem_limit_bytes=56 * 1024 * 1024
        ),
        name="routed_layer",
    )(
        ahead_rows[0].T, behind_rows[0].T, behind_grad[0].T, route_scores[0], route_counts[0], weights_in, weights_out
    )
    return (moved[0].T[None], moved[1].T[None])


def solution(mesh):
    in_specs = (
        P("section", None, "expert"),
        P("section", None, "expert"),
        P("section", None, "expert"),
        P("section", None, None),
        P("section", None),
        P("section", "expert", None, None, None),
        P("section", "expert", None, None),
    )
    out_specs = (P("section", None, "expert"), P("section", None, "expert"))
    step = functools.partial(body, mesh.shape["section"])
    return jax.shard_map(step, mesh=mesh, in_specs=in_specs, out_specs=out_specs, check_vma=False)
```

```python
import functools

import jax
import jax.numpy as jnp
from jax import lax
from jax.experimental import pallas as pl
from jax.experimental.pallas import tpu as pltpu
from jax.sharding import PartitionSpec as P

MESH = pl.DeviceIdType.MESH
DBLOCKS = 4
LINE = 4
CHUNK = 128
F32 = jnp.float32
BF16 = jnp.bfloat16


def layer_kernel(
    chunks, sections, ahead, behind, grad, scores, counts, gate_up, down, out_ahead, out_behind,
    w, xall, wt, pf, pb, rs_in, rl_out, actb, oacc, obf, y_in, zl_send, zr_send, zl_in, zr_in, fin, landed, fsum,
    w_sem, ag_send, ag_recv, rs_send, rs_recv, aq_send, aq_recv, y_send, y_recv, z_send, z_recv, s_send, s_recv,
):
    feats = ahead.shape[0]
    units = down.shape[0]
    half = units // (2 * DBLOCKS)
    me = lax.axis_index("expert")
    sec = lax.axis_index("section")
    devices = lax.axis_size("expert")
    col = me % 2
    z = me // 2
    line = z % LINE
    q = z // LINE
    q_up, q_down = (q + 1) % DBLOCKS, (q + 3) % DBLOCKS

    def expert(index):
        return {"expert": index % devices}

    right, left = expert(me + 2), expert(me + devices - 2)
    across = {"expert": z * 2 + (1 - col)}
    ahead_q, back_q = expert(me + 2 * LINE), expert(me + devices - 2 * LINE)
    sec_up = {"section": (sec + 1) % sections}
    sec_down = {"section": (sec + sections - 1) % sections}

    loads = [pltpu.make_async_copy(gate_up.at[k], w.at[k], w_sem.at[k]) for k in range(2)]
    loads.append(pltpu.make_async_copy(down, w.at[2], w_sem.at[2]))
    for load in loads:
        load.start()
    barrier = pltpu.get_barrier_semaphore()
    for peer in (right, left, across, ahead_q, back_q, sec_up, sec_down):
        pl.semaphore_signal(barrier, inc=1, device_id=peer, device_id_type=MESH)

    drains = []

    def remote(src, dst, send, recv, device):
        return pltpu.make_async_remote_copy(
            src_ref=src, dst_ref=dst, send_sem=send, recv_sem=recv, device_id=device, device_id_type=MESH
        )

    def post(copy, cond=None):
        if cond is None:
            copy.start()
        else:
            pl.when(cond)(lambda: copy.start())
        drains.append((copy, cond))

    def arrived(ref, recv):
        remote(ref, ref, recv, recv, across).wait_recv()

    def rows_of(position, column):
        return pl.ds(pl.multiple_of((position * 2 + column) * feats, 16), feats)

    def slot_of(position, column):
        return position * 2 + column

    def scale_of(m, j):
        slots = lax.broadcasted_iota(jnp.int32, (1, CHUNK), 1) + j * CHUNK
        return jnp.where(slots < counts[m], scores[m : m + 1, j * CHUNK : (j + 1) * CHUNK], 0.0)

    def place_own(j):
        slots = slice(j * CHUNK, (j + 1) * CHUNK)
        mine = rows_of(line, col)
        xall[j, mine, :CHUNK] = ahead[:, slots]
        xall[j, mine, CHUNK : 2 * CHUNK] = behind[:, slots]
        xall[j, mine, 2 * CHUNK :] = (grad[:, slots].astype(F32) * scale_of(1, j)).astype(BF16)

    def gather_own(j):
        spot = xall.at[j, rows_of(line, col), :]
        sem = ag_recv.at[j, slot_of(line, col)]
        post(remote(spot, spot, ag_send.at[j, 0], sem, right), line < LINE - 1)
        post(remote(spot, spot, ag_send.at[j, 1], sem, left), line > 0)
        post(remote(spot, spot, ag_send.at[j, 2], sem, across))

    def gather_step(j, t):
        for side in (0, 1):
            there = line >= t if side == 0 else line + t < LINE
            source = (line - t) & 3 if side == 0 else (line + t) & 3
            spot = xall.at[j, rows_of(source, col), :]
            sem = ag_recv.at[j, slot_of(source, col)]
            pl.when(there)(functools.partial(arrived, spot, sem))
            if t < LINE - 1:
                onward = jnp.logical_and(there, line < LINE - 1 if side == 0 else line > 0)
                post(remote(spot, spot, ag_send.at[j, 3 * t + side], sem, right if side == 0 else left), onward)
            post(remote(spot, spot, ag_send.at[j, 12 + 2 * t + side], sem, across), there)

    def gather_step1(j):
        gather_step(j, 1)

    def gather_step2(j):
        gather_step(j, 2)

    def gather_step3(j):
        gather_step(j, 3)

    def gather_rest(j):
        for position in range(LINE):
            arrived(xall.at[j, rows_of(position, 1 - col), :], ag_recv.at[j, slot_of(position, 1 - col)])

    def first_matmul(j):
        def keep(value, comp):
            for block in range(DBLOCKS):
                for part in range(2):
                    rows = value[(2 * block + part) * half : (2 * block + part + 1) * half]
                    pf[j, block, part, comp] = rows

        for k in range(2):
            value = jnp.dot(w[k], xall[j, :, : 2 * CHUNK], preferred_element_type=F32)
            keep(value[:, :CHUNK], k)
            keep(value[:, CHUNK:], 2 + k)
        keep(jnp.dot(w[2], xall[j, :, 2 * CHUNK :], preferred_element_type=F32), 4)

    def sums_start(j):
        far = (q + 2) % DBLOCKS
        for slot, block, part in ((0, q_up, 0), (1, far, 1), (2, far, 0), (3, q_down, 1)):
            pb[j, slot] = pf[j, block, part].astype(BF16)
        for way, device in ((0, ahead_q), (1, back_q)):
            pair = pl.ds(2 * way, 2)
            post(remote(pb.at[j, pair], rs_in.at[j, pair], rs_send.at[j, way], rs_recv.at[j, way], device))

    def sums_relay(j):
        for way, slot, block, part, device in ((0, 1, q_up, 1, ahead_q), (1, 2, q_down, 0, back_q)):
            arrived(rs_in.at[j, pl.ds(2 * way, 2)], rs_recv.at[j, way])
            rl_out[j, way] = (pf[j, block, part] + rs_in[j, slot].astype(F32)).astype(BF16)
            sems = rs_send.at[j, 2 + way], rs_recv.at[j, 2 + way]
            post(remote(rl_out.at[j, way], rs_in.at[j, 4 + way], *sems, device))

    def activate(j):
        for part, direct, relayed in ((0, 0, 5), (1, 3, 4)):
            arrived(rs_in.at[j, relayed], rs_recv.at[j, relayed - 2])
            total = pf[j, q, part] + rs_in[j, direct].astype(F32) + rs_in[j, relayed].astype(F32)
            gate_a, up_a, gate_b, up_b, expanded = [total[k] for k in range(5)]
            actb[j, q, part, 0] = (gate_a * jax.nn.sigmoid(gate_a) * up_a).astype(BF16)
            sg = jax.nn.sigmoid(gate_b)
            actb[j, q, part, 1] = (expanded * up_b * sg * (1.0 + gate_b * (1.0 - sg))).astype(BF16)
            actb[j, q, part, 2] = (expanded * gate_b * sg).astype(BF16)
        own = actb.at[j, q]
        post(remote(own, own, aq_send.at[j, 0], aq_recv.at[j, 0], ahead_q))
        post(remote(own, own, aq_send.at[j, 1], aq_recv.at[j, 1], back_q))

    def acts_relay(j):
        arrived(actb.at[j, q_down], aq_recv.at[j, 0])
        piece = actb.at[j, q_down, 0]
        post(remote(piece, piece, aq_send.at[j, 2], aq_recv.at[j, 2], ahead_q))
        arrived(actb.at[j, q_up], aq_recv.at[j, 1])
        piece = actb.at[j, q_up, 1]
        post(remote(piece, piece, aq_send.at[j, 3], aq_recv.at[j, 3], back_q))

    def second_matmul(j):
        far = (q + 2) % DBLOCKS
        arrived(actb.at[j, far, 0], aq_recv.at[j, 2])
        arrived(actb.at[j, far, 1], aq_recv.at[j, 3])
        acts = [actb[j, :, :, k].reshape(units, CHUNK) for k in range(3)]
        both = 2 * feats

        @pl.loop(0, LINE)
        def _(position):
            rows = pl.ds(pl.multiple_of(position * both, 16), both)
            ahead = jnp.dot(wt[2, rows, :], acts[0], preferred_element_type=F32)
            behind = jnp.dot(wt[0, rows, :], acts[1], preferred_element_type=F32)
            behind += jnp.dot(wt[1, rows, :], acts[2], preferred_element_type=F32)
            oacc[j, 0, rows, :] = ahead
            oacc[j, 1, rows, :] = behind
            obf[j, 0, rows, :] = ahead.astype(BF16)
            obf[j, 1, rows, :] = behind.astype(BF16)

        for position in (0, 3, 1, 2):
            post(
                remote(
                    obf.at[j, :, rows_of(position, 1 - col), :], y_in.at[j, position],
                    y_send.at[j, position], y_recv.at[j, position], across,
                )
            )

    def column_sum(j, position):
        return oacc[j, :, rows_of(position, col), :] + y_in[j, position].astype(F32)

    def scatter_line(j):
        for t in range(LINE - 1):
            scatter_target(j, t)

    def scatter_target(j, t):
        for side in (0, 1):
            target = LINE - 1 - t if side == 0 else t
            sends = line < target if side == 0 else line > target
            inner = line > 0 if side == 0 else line < LINE - 1
            joins = jnp.logical_and(sends, inner)
            landing, sending = (zr_in, zr_send) if side == 0 else (zl_in, zl_send)
            if t < LINE // 2:
                arrived(y_in.at[j, target], y_recv.at[j, target])

            @pl.when(jnp.logical_and(sends, jnp.logical_not(inner)))
            def _():
                sending[j, target] = column_sum(j, target).astype(BF16)

            @pl.when(joins)
            def _():
                arrived(landing.at[j, target], z_recv.at[j, side, target])
                sending[j, target] = (column_sum(j, target) + landing[j, target].astype(F32)).astype(BF16)

            post(
                remote(
                    sending.at[j, target], landing.at[j, target], z_send.at[j, side, target],
                    z_recv.at[j, side, target], right if side == 0 else left,
                ),
                sends,
            )

    def finish(j):
        fsum[...] = column_sum(j, line)
        for side in (0, 1):
            landing = zr_in if side == 0 else zl_in

            @pl.when(line > 0 if side == 0 else line < LINE - 1)
            def _():
                arrived(landing.at[j, line], z_recv.at[j, side, line])
                fsum[...] += landing[j, line].astype(F32)

        fin[j, 0] = (fsum[0] * scale_of(0, j)).astype(BF16)
        fin[j, 1] = fsum[1].astype(BF16)
        post(remote(fin.at[j, 0], landed.at[j, 0], s_send.at[j, 0], s_recv.at[j, 0], sec_up), sec < sections - 1)
        post(remote(fin.at[j, 1], landed.at[j, 1], s_send.at[j, 1], s_recv.at[j, 1], sec_down), sec > 0)

    def deliver(j):
        slots = slice(j * CHUNK, (j + 1) * CHUNK)
        for k, there, out in ((0, sec > 0, out_ahead), (1, sec < sections - 1, out_behind)):

            @pl.when(there)
            def _():
                arrived(landed.at[j, k], s_recv.at[j, k])
                out[:, slots] = landed[j, k]

            @pl.when(jnp.logical_not(there))
            def _():
                out[:, slots] = jnp.zeros((feats, CHUNK), BF16)

    def enter(j):
        gather_rest(j)
        first_matmul(j)
        sums_start(j)

    place_own(0)
    pl.semaphore_wait(barrier, 7)
    gather_own(0)
    place_own(1)
    gather_own(1)
    place_own(2)
    for k in range(3):
        loads[k].wait()
        wt[k] = w[k].T
    for step, j in (
        (gather_step1, 0), (gather_own, 2), (gather_step2, 0), (gather_step1, 1), (gather_step3, 0),
        (gather_step2, 1), (gather_step3, 1), (enter, 0), (gather_step1, 2), (gather_step2, 2), (enter, 1),
        (sums_relay, 0), (gather_step3, 2), (enter, 2), (sums_relay, 1), (activate, 0), (activate, 1),
        (acts_relay, 0), (sums_relay, 2), (acts_relay, 1), (second_matmul, 0), (activate, 2),
        (second_matmul, 1), (acts_relay, 2), (scatter_line, 0), (second_matmul, 2), (scatter_line, 1),
        (finish, 0), (scatter_line, 2), (finish, 1), (finish, 2), (deliver, 0), (deliver, 1), (deliver, 2),
    ):
        step(j)
    for copy, cond in drains:
        if cond is None:
            copy.wait_send()
        else:
            pl.when(cond)(lambda copy=copy: copy.wait_send())


def body(sections, ahead_rows, behind_rows, behind_grad, route_scores, route_counts, gate_up, down_proj):
    weights_in = gate_up[0, 0]
    weights_out = down_proj[0, 0]
    _, units, width = weights_in.shape
    slots, feats = ahead_rows.shape[1:]
    chunks = slots // CHUNK
    half = units // (2 * DBLOCKS)
    vmem = pl.BlockSpec(memory_space=pltpu.VMEM)
    smem = pl.BlockSpec(memory_space=pltpu.SMEM)
    here = pl.BlockSpec(memory_space=pl.ANY)
    dma = pltpu.SemaphoreType.DMA
    out = jax.ShapeDtypeStruct((feats, slots), BF16)
    piece = (5, half, CHUNK)
    moved = pl.pallas_call(
        functools.partial(layer_kernel, chunks, sections),
        out_shape=(out, out),
        in_specs=[vmem, vmem, vmem, vmem, smem, here, here],
        out_specs=(vmem, vmem),
        scratch_shapes=[
            pltpu.VMEM((3, units, width), BF16),
            pltpu.VMEM((chunks, width, 3 * CHUNK), BF16),
            pltpu.VMEM((3, width, units), BF16),
            pltpu.VMEM((chunks, DBLOCKS, 2) + piece, F32),
            pltpu.VMEM((chunks, 4) + piece, BF16),
            pltpu.VMEM((chunks, 6) + piece, BF16),
            pltpu.VMEM((chunks, 2) + piece, BF16),
            pltpu.VMEM((chunks, DBLOCKS, 2, 3, half, CHUNK), BF16),
            pltpu.VMEM((chunks, 2, width, CHUNK), F32),
            pltpu.VMEM((chunks, 2, width, CHUNK), BF16),
            pltpu.VMEM((chunks, LINE, 2, feats, CHUNK), BF16),
            pltpu.VMEM((chunks, LINE, 2, feats, CHUNK), BF16),
            pltpu.VMEM((chunks, LINE, 2, feats, CHUNK), BF16),
            pltpu.VMEM((chunks, LINE, 2, feats, CHUNK), BF16),
            pltpu.VMEM((chunks, LINE, 2, feats, CHUNK), BF16),
            pltpu.VMEM((chunks, 2, feats, CHUNK), BF16),
            pltpu.VMEM((chunks, 2, feats, CHUNK), BF16),
            pltpu.VMEM((2, feats, CHUNK), F32),
            dma((3,)),
            dma((chunks, 20)),
            dma((chunks, 2 * LINE)),
            dma((chunks, 4)),
            dma((chunks, 4)),
            dma((chunks, 4)),
            dma((chunks, 4)),
            dma((chunks, LINE)),
            dma((chunks, LINE)),
            dma((chunks, 2, LINE)),
            dma((chunks, 2, LINE)),
            dma((chunks, 2)),
            dma((chunks, 2)),
        ],
        compiler_params=pltpu.CompilerParams(
            collective_id=0, has_side_effects=True, vmem_limit_bytes=56 * 1024 * 1024
        ),
        name="routed_layer",
    )(
        ahead_rows[0].T, behind_rows[0].T, behind_grad[0].T, route_scores[0], route_counts[0], weights_in, weights_out
    )
    sec = lax.axis_index("section")
    got_ahead = jnp.where(sec > 0, moved[0], jnp.zeros_like(moved[0]))
    got_behind = jnp.where(sec < sections - 1, moved[1], jnp.zeros_like(moved[1]))
    return (got_ahead.T[None], got_behind.T[None])


def solution(mesh):
    in_specs = (
        P("section", None, "expert"),
        P("section", None, "expert"),
        P("section", None, "expert"),
        P("section", None, None),
        P("section", None),
        P("section", "expert", None, None, None),
        P("section", "expert", None, None),
    )
    out_specs = (P("section", None, "expert"), P("section", None, "expert"))
    step = functools.partial(body, mesh.shape["section"])
    return jax.shard_map(step, mesh=mesh, in_specs=in_specs, out_specs=out_specs, check_vma=False)
```
